32 devices in a mesh: dp: 16 (over z, y, x), mp: 2 (over core).
Axes of the slice: x: 2, y: 2, z: 4, core: 2. Of those that a mesh axis runs over, the one named last changes fastest.
Arguments:
- store_rows: bfloat16 [8192, 4096], P('dp', 'mp'), may hold values from -64 to 64
- norm_gain: bfloat16 [4096], replicated, may hold values from 0.099609375 to 1.8984375
- key_weight: bfloat16 [4096, 2048], P(None, 'mp'), may hold values from -0.09375 to 0.09375
- value_weight: bfloat16 [4096, 2048], P(None, 'mp'), may hold values from -0.09375 to 0.09375
- queries: bfloat16 [128, 2048], P('dp', 'mp'), may hold values from -300 to 300
- counts: int32 [16], replicated, may hold values from 1 to 8, 32 in all
- slot_plan: int32 [32], P('dp'), may hold values from 0 to 31, each once
Outputs:
- context: bfloat16 [128, 2048], P('dp', 'mp')
The draws below stay inside these ranges and needn't reach their ends.
All inputs are finite; a program needn't handle non-finite values.
Results may differ from the reference program's by a relative error of at most 0.0091.
Values may be sent and summed in bfloat16 or wider, within the bound.
A program may use at most 64 MiB of HBM per device.

```python
import math
import jax
import jax.numpy as jnp
import numpy as np
from jax import lax

D = 4096
HEADS = 32
HEAD_DIM = 64
PASSAGE_LEN = 256
MOST = 8
DEC = 8
QUESTIONS = 16
PASSAGES = 32


def draw_store_rows(key, part):
    first_key, second_key, third_key = jax.random.split(key, 3)
    row_total = PASSAGES * PASSAGE_LEN
    column_pos = jnp.arange(D, dtype=jnp.float32) / D
    column_scale = 0.5 * jnp.power(3.0, column_pos) * jnp.exp(jax.random.uniform(second_key, (D,), jnp.float32, -0.35, 0.35))
    row_scale = jnp.exp(jax.random.uniform(third_key, (row_total, 1), jnp.float32, 0.0, math.log(10.0)))
    base_rows = jax.random.normal(first_key, (row_total, D), jnp.float32)
    return jnp.clip(base_rows * row_scale * column_scale[None, :], -64.0, 64.0).astype(jnp.bfloat16)


def draw_queries(key, part):
    first_key = jax.random.fold_in(key, 0)
    row_total = QUESTIONS * DEC
    column_total = HEADS * HEAD_DIM
    base_rows = jax.random.normal(first_key, (row_total, column_total), jnp.float32) * 2.5
    return jnp.clip(base_rows, -300.0, 300.0).astype(jnp.bfloat16)


def levels(rng, shape, cuts, smallest, high):
    def one(axis_at, parts):
        heights = jax.random.uniform(jax.random.fold_in(jax.random.fold_in(rng, 6), axis_at), (parts,), jnp.float32, smallest / len(cuts), high / len(cuts))
        return jnp.repeat(jnp.exp(heights), shape[axis_at] // parts).reshape((-1,) + (1,) * (len(shape) - axis_at - 1))

    level = one(*cuts[0])
    for cut in cuts[1:]:
        level = level * one(*cut)
    return level


def length_profile(count, total, most, skew):
    weights = [(1 << 20) // math.isqrt(grade ** skew) + 1 for grade in range(2, count + 1)]
    spare, holding = total - most - (count - 1), [1] * (count - 1)
    while spare > 0:
        movable = [i for i in range(count - 1) if holding[i] < most]
        pool, left = sum([weights[i] for i in movable]), spare
        for i in movable:
            addition = min(most - holding[i], max(1, left * weights[i] // pool), spare)
            holding[i] = holding[i] + addition
            spare = spare - addition
    return np.array([most] + holding)


def uneven(own_key, count, total, most, lean):
    if count == 2:
        one = jax.random.randint(own_key, (), max(1, total - most), min(most, total - 1) + 1)
        return jnp.stack([one, total - one])
    sizes = jnp.asarray(length_profile(count, total, most, lean), jnp.int32)
    pairs = (count - 1) // 2
    donor, receiver = sizes[1:1 + 2 * pairs:2], sizes[2:2 + 2 * pairs:2]
    room = jnp.minimum(donor - 1, most - receiver)
    passed = jax.random.randint(jax.random.fold_in(own_key, 1), (pairs,), 0, 1 << 20) % (room + 1)
    sizes = sizes.at[1:1 + 2 * pairs:2].set(donor - passed).at[2:2 + 2 * pairs:2].set(receiver + passed)
    return sizes[jax.random.permutation(jax.random.fold_in(own_key, 2), count)]


def normal_values(key, extent, spread, reach, cuts=(), kind=jnp.bfloat16):
    result = spread * jax.random.normal(key, extent, jnp.float32)
    if cuts:
        result = result * levels(key, extent, cuts, -0.22, 0.18)
    return jnp.clip(result, -reach, reach).astype(kind)


def setup_inputs(seed: int = 0) -> dict:
    keys = jax.random.split(jax.random.key(seed), 8)
    return {
        "store_rows": draw_store_rows(jax.random.fold_in(keys[7], 71), 0),
        "norm_gain": jnp.clip(1.0 + 0.18 * jax.random.normal(keys[1], (D,), jnp.float32), 0.099609375, 1.8984375).astype(jnp.bfloat16),
        "key_weight": normal_values(keys[2], (D, HEADS * HEAD_DIM), D ** -0.5, 0.09375, ((1, 2),)),
        "value_weight": normal_values(keys[3], (D, HEADS * HEAD_DIM), D ** -0.5, 0.09375, ((1, 2),)),
        "queries": draw_queries(jax.random.fold_in(keys[7], 71), 0),
        "counts": uneven(keys[5], QUESTIONS, PASSAGES, MOST, 2).astype(jnp.int32),
        "slot_plan": jax.random.permutation(keys[6], PASSAGES).astype(jnp.int32),
    }


norm_eps = 1e-06
score_scale = 0.125
far_below = -1e+30

def reference(store_rows, norm_gain, key_weight, value_weight, queries, counts, slot_plan):
    row_blocks = store_rows.reshape(PASSAGES, PASSAGE_LEN, D)
    gain_full = norm_gain.astype(jnp.float32)

    def project(row_block):
        raw_rows = row_block.astype(jnp.float32)
        inv_rms = lax.rsqrt(lax.optimization_barrier(jnp.mean(raw_rows * raw_rows, axis=1, keepdims=True)) + norm_eps)
        scaled = (raw_rows * gain_full[None, :]).astype(jnp.bfloat16)
        key_rows = (jnp.dot(scaled, key_weight, preferred_element_type=jnp.float32) * inv_rms).astype(jnp.bfloat16)
        value_rows = (jnp.dot(scaled, value_weight, preferred_element_type=jnp.float32) * inv_rms).astype(jnp.bfloat16)
        return (key_rows, value_rows)
    all_keys, all_values = lax.map(project, row_blocks)
    ends = jnp.cumsum(counts)
    slot_question = lax.optimization_barrier(jnp.sum((slot_plan[:, None] >= ends[None, :]).astype(jnp.int32), axis=1))
    query_table = queries.reshape(QUESTIONS, DEC, HEADS, HEAD_DIM)

    def scores_of(key_block, question):
        own_queries = jnp.take(query_table, question, axis=0).astype(jnp.float32)
        key_heads = key_block.reshape(PASSAGE_LEN, HEADS, HEAD_DIM).astype(jnp.float32)
        return jnp.einsum('ihd,thd->hit', own_queries, key_heads, precision=lax.Precision.HIGHEST) * score_scale

    def slot_peak(slot_item):
        return lax.optimization_barrier(jnp.max(scores_of(slot_item[0], slot_item[1]), axis=2))
    slot_max = lax.map(slot_peak, (all_keys, slot_question))
    member = slot_question[None, :] == jnp.arange(QUESTIONS, dtype=jnp.int32)[:, None]
    question_max = lax.optimization_barrier(jnp.max(jnp.where(member[:, :, None, None], slot_max[None], far_below), axis=1))

    def slot_terms(slot_item):
        key_block, value_block, question = slot_item
        scores = scores_of(key_block, question)
        weights = jnp.exp(scores - question_max[question][:, :, None])
        value_heads = value_block.reshape(PASSAGE_LEN, HEADS, HEAD_DIM).astype(jnp.float32)
        slot_num = jnp.einsum('hit,thd->hid', weights, value_heads, precision=lax.Precision.HIGHEST)
        return (slot_num, lax.optimization_barrier(jnp.sum(weights, axis=2)))
    slot_num, slot_den = lax.map(slot_terms, (all_keys, all_values, slot_question))
    numerator = jax.ops.segment_sum(slot_num, slot_question, num_segments=QUESTIONS)
    denominator = jax.ops.segment_sum(slot_den, slot_question, num_segments=QUESTIONS)
    context = numerator / denominator[..., None]
    return jnp.transpose(context, (0, 2, 1, 3)).reshape(QUESTIONS * DEC, HEADS * HEAD_DIM).astype(jnp.bfloat16)
```

```python
import functools

import jax
import jax.numpy as jnp
from jax import lax
from jax.experimental import pallas as pl
from jax.experimental.pallas import tpu as pltpu
from jax.sharding import PartitionSpec as P

HEAD_DIM = 64
MESH = pl.DeviceIdType.MESH
bf16, f32 = jnp.bfloat16, jnp.float32

norm_eps = 1e-06
score_scale = 0.125
far_below = -1e30
STAT = 128
PIECE = 32


def body(dims, counts_hbm, plan_hbm, gain_hbm, queries_hbm, rows_hbm, key_hbm, value_hbm, out,
         counts, plan, gain, raw, xs, wbuf, acc, kvb, sums, qbuf, own, msg, got,
         small_sem, rows_sem, w_sem, xsend, xrecv, ssend, srecv, qsend, qrecv, msend, mrecv):
    dp, mp, row_count, feats, cols, piece, width, sends, questions, dec, passages = dims
    full = feats * mp
    seq = row_count // passages
    pieces = feats // piece
    groups = cols // width
    gheads = width // HEAD_DIM
    tall = gheads * dec
    per_send = groups // sends
    send_width = cols // sends
    me = lax.axis_index("dp")
    core = lax.axis_index("mp")
    weights = (key_hbm, value_hbm)
    lines = dp // 4
    me_line, me_y, me_x = lax.div(me, 4), lax.rem(lax.div(me, 2), 2), lax.rem(me, 2)

    def other(j, way):
        line = lax.rem(me_line + (lines - j // 4 if way < 0 else j // 4), lines)
        return line * 4 + lax.rem(me_y + j // 2, 2) * 2 + lax.rem(me_x + j, 2)

    def slot_from(sender):
        line = lax.rem(lax.div(sender, 4) - me_line + lines, lines)
        return line * 4 + lax.rem(lax.rem(lax.div(sender, 2), 2) + me_y, 2) * 2 + lax.rem(lax.rem(sender, 2) + me_x, 2)

    barrier = pltpu.get_barrier_semaphore()
    for s in range(1, mp):
        pl.semaphore_signal(barrier, inc=1, device_id=(me, lax.rem(core + s, mp)), device_id_type=MESH)

    def announce(j, carry):
        pl.semaphore_signal(barrier, inc=1, device_id=(lax.rem(me + j, dp), core), device_id_type=MESH)
        return carry

    lax.fori_loop(1, dp, announce, 0, unroll=dp <= 16)

    def rows_copy(k):
        at = pl.ds(k * piece, piece)
        return pltpu.make_async_copy(rows_hbm.at[:, at], raw.at[k], rows_sem.at[k])

    def weight_copy(s, c, k):
        start = pl.multiple_of(lax.rem(core + s, mp) * feats + k * piece, piece)
        return pltpu.make_async_copy(weights[c].at[pl.ds(start, piece), :], wbuf.at[s, c, k], w_sem.at[s, c, k])

    order = [(s, c, k) for s in range(mp) for c in range(2) for k in range(pieces)]

    def fetched(s, c, k):
        weight_copy(s, c, k).wait()
        ahead = order.index((s, c, k)) + WINDOW
        if ahead < len(order):
            weight_copy(*order[ahead]).start()

    small = [pltpu.make_async_copy(gain_hbm, gain, small_sem.at[0]),
             pltpu.make_async_copy(counts_hbm, counts, small_sem.at[1]),
             pltpu.make_async_copy(plan_hbm, plan, small_sem.at[2])]
    for h in range(sends):
        small.append(pltpu.make_async_copy(
            queries_hbm.at[:, pl.ds(h * send_width, send_width)], qbuf.at[h, 0], small_sem.at[3 + h]))
    small[0].start()
    for k in range(pieces):
        rows_copy(k).start()
    for step in order[:FIRST]:
        weight_copy(*step).start()
    for copy in small[1:]:
        copy.start()

    small[0].wait()

    def scale(k):
        rows_copy(k).wait()
        if k == pieces - 1:
            for step in order[FIRST:WINDOW]:
                weight_copy(*step).start()
        start = pl.multiple_of(core * feats + k * piece, piece)
        own_gain = gain[pl.ds(start, piece)].reshape(1, piece)
        x = raw[k]
        xs[0, k] = x * own_gain

    def square(k):
        x = raw[k].astype(f32)
        x = x * x
        total = x[:, :128]
        for lanes in range(128, piece, 128):
            total = total + x[:, lanes:lanes + 128]
        sums[0] = total if k == 0 else sums[0] + total

    def x_copy(s, k):
        return pltpu.make_async_remote_copy(
            src_ref=xs.at[0, k], dst_ref=xs.at[s, k], send_sem=xsend.at[s, k], recv_sem=xrecv.at[s, k],
            device_id=(me, lax.rem(core + mp - s, mp)), device_id_type=MESH)

    def sum_copy(s):
        return pltpu.make_async_remote_copy(
            src_ref=sums.at[0], dst_ref=sums.at[s], send_sem=ssend.at[s], recv_sem=srecv.at[s],
            device_id=(me, lax.rem(core + mp - s, mp)), device_id_type=MESH)

    def q_copy(h, j):
        return pltpu.make_async_remote_copy(
            src_ref=qbuf.at[h, 0], dst_ref=qbuf.at[h, j], send_sem=qsend.at[h], recv_sem=qrecv.at[h],
            device_id=(other(j, -1), core), device_id_type=MESH)

    def start_queries():
        for h in range(sends):
            small[3 + h].wait()
        pl.semaphore_wait(barrier, dp - 1 + mp - 1)
        for h in range(sends):
            lax.fori_loop(1, dp, lambda j, carry: (q_copy(h, dp - j).start(), carry)[1], 0, unroll=dp <= 16)

    def product(s, c):
        total = None
        for k in range(pieces):
            fetched(s, c, k)
            if s > 0 and c == 0:
                x_copy(s, k).wait()
            term = jnp.dot(xs[s, k], wbuf[s, c, k], preferred_element_type=f32)
            total = term if total is None else total + term
            if s == 0 and c == 0:
                if k == min(BARRIER_AT, pieces - 1):
                    start_queries()
                for o in range(1, mp):
                    if k == min(BARRIER_AT, pieces - 1):
                        for e in range(k + 1):
                            x_copy(o, e).start()
                    elif k > BARRIER_AT:
                        x_copy(o, k).start()
        return total

    for k in range(pieces):
        scale(k)
        square(k)
    for c in range(2):
        acc[c] = product(0, c)
        if c == 0:
            for s in range(1, mp):
                sum_copy(s).start()

    across = (((1,), (1,)), ((), ()))
    slot = []
    small[1].wait()
    small[2].wait()
    for p in range(passages):
        plan_p = plan[p]

        def count(q, carry):
            end, before = carry
            end = end + counts[q]
            return end, before + jnp.where(end <= plan_p, 1, 0)

        found = lax.fori_loop(0, questions, count, (jnp.int32(0), jnp.int32(0)), unroll=8)[1]
        slot.append(jnp.minimum(found, questions - 1))

    for s in range(1, mp):
        if s == mp - 1:
            for o in range(1, mp):
                sum_copy(o).wait()
            total = sums[0]
            for o in range(1, mp):
                total = total + sums[o]
            high = total.astype(bf16)
            low = (total - high.astype(f32)).astype(bf16)
            both = jnp.concatenate([high, low], axis=1)
            ones = jnp.ones((256, 128), bf16)
            inv_rms = lax.rsqrt(jnp.dot(both, ones, preferred_element_type=f32) * (1.0 / full) + norm_eps)
            total = lax.dot_general(jnp.ones((8, 256), bf16), both, across, preferred_element_type=f32)
            inv_row = lax.rsqrt(total * (1.0 / full) + norm_eps)[0:1]
        for c in range(2):
            total = product(s, c) + acc[c]
            if s < mp - 1:
                acc[c] = total
            elif c == 1:
                kvb[c] = total.astype(bf16)
            else:
                for lanes in range(0, cols, 128):
                    kvb[c, :, lanes:lanes + 128] = (total[:, lanes:lanes + 128] * inv_rms).astype(bf16)

    row_head = lax.broadcasted_iota(jnp.int32, (tall, width), 0) // dec
    col_head = lax.broadcasted_iota(jnp.int32, (tall, width), 1) // HEAD_DIM
    diagonal = row_head == col_head
    stat_row = lax.broadcasted_iota(jnp.int32, (tall, STAT), 0) // dec
    stat_head = lax.rem(lax.broadcasted_iota(jnp.int32, (tall, STAT), 1), PIECE)
    stat_piece = lax.broadcasted_iota(jnp.int32, (dec, STAT), 1) // PIECE

    def attend(p, g):
        at = slice(g * width, (g + 1) * width)
        h = g // per_send
        q = qbuf[h, slot_from(slot[p]), :, (g - h * per_send) * width:(g + 1 - h * per_send) * width]
        q = jnp.where(diagonal, jnp.concatenate([q.astype(f32)] * gheads, axis=0), 0.0).astype(bf16)
        k = kvb[0, p * seq:(p + 1) * seq, at]
        scores = lax.dot_general(q, k, across, preferred_element_type=f32) * score_scale
        level = jnp.max(scores, axis=1, keepdims=True)
        w = jnp.exp(scores - level)
        den = jnp.sum(w, axis=1, keepdims=True)
        v = kvb[1, p * seq:(p + 1) * seq, at]
        num = jnp.dot((w * inv_row[:, p * seq:(p + 1) * seq]).astype(bf16), v, preferred_element_type=f32)
        return level, den, num

    def gather(parts, p):
        level, den, num = parts[p]
        top = level
        for o in range(p + 1, passages):
            top = jnp.where(slot[o] == slot[p], jnp.maximum(top, parts[o][0]), top)
        scale = jnp.exp(level - top)
        den = den * scale
        num = num * scale
        for o in range(p + 1, passages):
            scale = jnp.where(slot[o] == slot[p], jnp.exp(jnp.minimum(parts[o][0] - top, 0.0)), 0.0)
            den = den + parts[o][1] * scale
            num = num + parts[o][2] * scale
        num = jnp.where(diagonal, num * (1.0 / den), 0.0)
        num = jnp.sum(num.reshape(gheads, dec, width), axis=0)
        return num, jnp.broadcast_to(top + jnp.log(den), (tall, STAT))

    def pieces_of(x):
        high = x.astype(bf16).astype(f32)
        rest = x - high
        middle = rest.astype(bf16).astype(f32)
        return jnp.where(stat_piece == 0, high, jnp.where(stat_piece == 1, middle, rest - middle))

    def m_copy(h, j):
        return pltpu.make_async_remote_copy(
            src_ref=msg.at[h, j - 1], dst_ref=got.at[h, j - 1], send_sem=msend.at[h], recv_sem=mrecv.at[h],
            device_id=(other(j, -1), core), device_id_type=MESH)

    for h in range(sends):
        own[h, passages, :, :send_width] = jnp.zeros((dec, send_width), bf16)
        own[h, passages, :, send_width:] = pieces_of(jnp.full((dec, STAT), far_below, f32)).astype(bf16)

    def pick_own(h, target):
        at = jnp.int32(passages)
        for p in reversed(range(passages)):
            at = jnp.where(slot[p] == target, p, at)
        return own[h, at]

    for h in range(sends):
        others = qbuf.at[h, pl.ds(1, dp - 1)]
        pltpu.make_async_copy(others, others, qrecv.at[h]).wait()
        nums = [[] for _ in range(passages)]
        stats = [jnp.zeros((dec, STAT), f32) for _ in range(passages)]
        for g in range(h * per_send, (h + 1) * per_send):
            parts = [attend(p, g) for p in range(passages)]
            for p in range(passages):
                num, lse = gather(parts, p)
                nums[p].append(num.astype(bf16))
                put = stat_head == stat_row + g * gheads
                stats[p] = stats[p] + jnp.sum(jnp.where(put, lse, 0.0).reshape(gheads, dec, STAT), axis=0)
        nums = [jnp.concatenate(n, axis=1) for n in nums]
        stats = [pieces_of(x).astype(bf16) for x in stats]
        for p in range(passages):
            own[h, p, :, :send_width] = nums[p]
            own[h, p, :, send_width:] = stats[p]

        def send(j, carry):
            msg[h, dp - j - 1] = pick_own(h, other(dp - j, -1))
            m_copy(h, dp - j).start()
            return carry

        lax.fori_loop(1, dp, send, 0, unroll=5 if dp == 16 else 3)
        got[h, dp - 1] = pick_own(h, me)

    pick_row = lax.rem(lax.broadcasted_iota(jnp.int32, (2 * STAT, send_width), 0), STAT)
    pick_col = lax.broadcasted_iota(jnp.int32, (2 * STAT, send_width), 1) // HEAD_DIM
    for h in range(sends):
        arrived = got.at[h, pl.ds(0, dp - 1)]
        pltpu.make_async_copy(arrived, arrived, mrecv.at[h]).wait()
        stat = got[h, :, :, send_width:].astype(f32).reshape(dp * dec, STAT)
        lse = stat + pltpu.roll(stat, STAT - PIECE, 1) + pltpu.roll(stat, STAT - 2 * PIECE, 1)
        lse = lse.reshape(dp, dec, STAT)
        hit = lse > 0.5 * far_below
        top = jnp.max(lse, axis=0, keepdims=True)
        w = jnp.where(hit, jnp.exp(lse - top), 0.0)
        den = jnp.sum(w, axis=0, keepdims=True)
        share = (w / jnp.where(den > 0.0, den, 1.0)).reshape(dp * dec, STAT)
        high = share.astype(bf16)
        low = (share - high.astype(f32)).astype(bf16)
        pick = jnp.where(pick_row == pick_col + h * (send_width // HEAD_DIM), 1.0, 0.0).astype(bf16)
        spread = jnp.dot(jnp.concatenate([high, low], axis=1), pick, preferred_element_type=f32)
        nums = got[h, :, :, :send_width].astype(f32)
        out[:, h * send_width:(h + 1) * send_width] = jnp.sum(spread.reshape(dp, dec, send_width) * nums, axis=0).astype(bf16)

    for h in range(sends):
        others = qbuf.at[h, pl.ds(1, dp - 1)]
        pltpu.make_async_copy(others, others, qsend.at[h]).wait()
    for h in range(sends):
        sent = msg.at[h]
        pltpu.make_async_copy(sent, sent, msend.at[h]).wait()


BARRIER_AT = 0
WINDOW = 4
FIRST = 2
SENDS = 1


def local(dp, mp, store_rows, norm_gain, key_weight, value_weight, queries, counts, slot_plan):
    row_count, feats = store_rows.shape
    cols = key_weight.shape[1]
    width = min(256, cols)
    sends = min(SENDS, cols // width)
    piece = min(512, feats)
    pieces = feats // piece
    passages = slot_plan.shape[0]
    dec = queries.shape[0]
    questions = counts.shape[0]
    dims = (dp, mp, row_count, feats, cols, piece, width, sends, questions, dec, passages)
    vmem = pl.BlockSpec(memory_space=pltpu.VMEM)
    hbm = pl.BlockSpec(memory_space=pl.ANY)
    dma = pltpu.SemaphoreType.DMA
    line = cols // sends + STAT
    return pl.pallas_call(
        functools.partial(body, dims),
        out_shape=jax.ShapeDtypeStruct((dec, cols), bf16),
        in_specs=[hbm] * 7,
        out_specs=vmem,
        scratch_shapes=[
            pltpu.SMEM((questions,), jnp.int32),
            pltpu.SMEM((passages,), jnp.int32),
            pltpu.VMEM((feats * mp,), bf16),
            pltpu.VMEM((pieces, row_count, piece), bf16),
            pltpu.VMEM((mp, pieces, row_count, piece), bf16),
            pltpu.VMEM((mp, 2, pieces, piece, cols), bf16),
            pltpu.VMEM((2, row_count, cols), f32),
            pltpu.VMEM((2, row_count, cols), bf16),
            pltpu.VMEM((mp, row_count, 128), f32),
            pltpu.VMEM((sends, dp, dec, cols // sends), bf16),
            pltpu.VMEM((sends, passages + 1, dec, line), bf16),
            pltpu.VMEM((sends, dp - 1, dec, line), bf16),
            pltpu.VMEM((sends, dp, dec, line), bf16),
            dma((3 + sends,)),
            dma((pieces,)),
            dma((mp, 2, pieces)),
            dma((mp, pieces)),
            dma((mp, pieces)),
            dma((mp,)),
            dma((mp,)),
            dma((sends,)),
            dma((sends,)),
            dma((sends,)),
            dma((sends,)),
        ],
        compiler_params=pltpu.CompilerParams(
            collective_id=0, has_side_effects=True, vmem_limit_bytes=56 * 1024 * 1024),
    )(counts, slot_plan, norm_gain, queries, store_rows, key_weight, value_weight)


def solution(mesh):
    placed = (P("dp", "mp"), P(), P(None, "mp"), P(None, "mp"), P("dp", "mp"), P(), P("dp"))
    return jax.shard_map(
        functools.partial(local, mesh.shape["dp"], mesh.shape["mp"]),
        mesh=mesh, in_specs=placed, out_specs=P("dp", "mp"), check_vma=False
    )
```

```python
import functools

import jax
import jax.numpy as jnp
from jax import lax
from jax.experimental import pallas as pl
from jax.experimental.pallas import tpu as pltpu
from jax.sharding import PartitionSpec as P

HEAD_DIM = 64
MESH = pl.DeviceIdType.MESH
bf16, f32 = jnp.bfloat16, jnp.float32

norm_eps = 1e-06
score_scale = 0.125
far_below = -1e30
HEADS_MOST = 16


def body(dims, counts_hbm, plan_hbm, gain_hbm, queries_hbm, rows_hbm, key_hbm, value_hbm, out,
         counts, plan, gain, raw, xs, wbuf, acc, kvb, sums, qbuf, own, msg, got,
         small_sem, rows_sem, w_sem, xsend, xrecv, ssend, srecv, qsend, qrecv, msend, mrecv):
    dp, mp, row_count, feats, cols, piece, width, questions, dec, passages = dims
    full = feats * mp
    seq = row_count // passages
    pieces = feats // piece
    groups = cols // width
    gheads = width // HEAD_DIM
    tall = gheads * dec
    me = lax.axis_index("dp")
    core = lax.axis_index("mp")
    weights = (key_hbm, value_hbm)
    lines = dp // 4
    me_line, me_y, me_x = lax.div(me, 4), lax.rem(lax.div(me, 2), 2), lax.rem(me, 2)

    def other(j, way):
        line = lax.rem(me_line + (lines - j // 4 if way < 0 else j // 4), lines)
        return line * 4 + lax.rem(me_y + j // 2, 2) * 2 + lax.rem(me_x + j, 2)

    def slot_to(target):
        line = lax.rem(me_line - lax.div(target, 4) + lines, lines)
        return line * 4 + lax.rem(lax.rem(lax.div(target, 2), 2) + me_y, 2) * 2 + lax.rem(lax.rem(target, 2) + me_x, 2)

    def slot_from(sender):
        line = lax.rem(lax.div(sender, 4) - me_line + lines, lines)
        return line * 4 + lax.rem(lax.rem(lax.div(sender, 2), 2) + me_y, 2) * 2 + lax.rem(lax.rem(sender, 2) + me_x, 2)

    barrier = pltpu.get_barrier_semaphore()
    for s in range(1, mp):
        pl.semaphore_signal(barrier, inc=1, device_id=(me, lax.rem(core + s, mp)), device_id_type=MESH)

    def announce(j, carry):
        pl.semaphore_signal(barrier, inc=1, device_id=(lax.rem(me + j, dp), core), device_id_type=MESH)
        return carry

    lax.fori_loop(1, dp, announce, 0, unroll=dp <= 16)

    def rows_copy(k):
        at = pl.ds(k * piece, piece)
        return pltpu.make_async_copy(rows_hbm.at[:, at], raw.at[k], rows_sem.at[k])

    def weight_copy(s, c, k):
        start = pl.multiple_of(lax.rem(core + s, mp) * feats + k * piece, piece)
        return pltpu.make_async_copy(weights[c].at[pl.ds(start, piece), :], wbuf.at[s, c, k], w_sem.at[s, c, k])

    order = [(s, c, k) for s in range(mp) for c in range(2) for k in range(pieces)]

    def fetched(s, c, k):
        weight_copy(s, c, k).wait()
        start_to(order.index((s, c, k)) + 1 + pieces + WINDOW)

    small = [pltpu.make_async_copy(gain_hbm, gain, small_sem.at[0]),
             pltpu.make_async_copy(counts_hbm, counts, small_sem.at[1]),
             pltpu.make_async_copy(plan_hbm, plan, small_sem.at[2])]
    small.append(pltpu.make_async_copy(queries_hbm, qbuf.at[0], small_sem.at[3]))
    small[0].start()
    loads = []
    for k in range(pieces):
        loads += [rows_copy(k), weight_copy(*order[k])]
    if ROWS_FIRST:
        loads = loads[::2] + loads[1::2]
    loads += [weight_copy(*step) for step in order[pieces:]]
    started = [0]

    def start_to(count):
        for copy in loads[started[0]:count]:
            copy.start()
        started[0] = max(started[0], min(count, len(loads)))

    start_to(FIRST)
    for copy in small[1:]:
        copy.start()

    small[0].wait()

    def scale(k):
        rows_copy(k).wait()
        start_to(FIRST + 1 + k)
        start = pl.multiple_of(core * feats + k * piece, piece)
        own_gain = gain[pl.ds(start, piece)].reshape(1, piece)
        x = raw[k]
        xs[0, k] = x * own_gain

    def square(k):
        x = raw[k].astype(f32)
        x = x * x
        total = x[:, :128]
        for lanes in range(128, piece, 128):
            total = total + x[:, lanes:lanes + 128]
        sums[0] = total if k == 0 else sums[0] + total

    def x_copy(s, k):
        return pltpu.make_async_remote_copy(
            src_ref=xs.at[0, k], dst_ref=xs.at[s, k], send_sem=xsend.at[s, k], recv_sem=xrecv.at[s, k],
            device_id=(me, lax.rem(core + mp - s, mp)), device_id_type=MESH)

    def sum_copy(s):
        return pltpu.make_async_remote_copy(
            src_ref=sums.at[0], dst_ref=sums.at[s], send_sem=ssend.at[s], recv_sem=srecv.at[s],
            device_id=(me, lax.rem(core + mp - s, mp)), device_id_type=MESH)

    def q_copy(j):
        return pltpu.make_async_remote_copy(
            src_ref=qbuf.at[0], dst_ref=qbuf.at[j], send_sem=qsend, recv_sem=qrecv,
            device_id=(other(j, -1), core), device_id_type=MESH)

    def q_slot(i):
        if Q_ORDER == 0:
            return dp - i
        if Q_ORDER == 1:
            return slot_to(jnp.where(i - 1 < me, i - 1, i))
        if Q_ORDER == 2:
            return slot_to(jnp.where(dp - i <= me, dp - i - 1, dp - i))
        return (lines - 1 - (dp - i) // 4) * 4 + 4 + (dp - i) % 4 if (dp - i) >= 4 else dp - i

    def start_queries():
        small[3].wait()
        pl.semaphore_wait(barrier, dp - 1 + mp - 1)
        lax.fori_loop(1, dp, lambda j, carry: (q_copy(q_slot(j)).start(), carry)[1], 0, unroll=dp <= 16)

    def product(s, c):
        total = None
        if s + c >= TOGETHER:
            for k in range(pieces):
                fetched(s, c, k)
                if s > 0 and c == 0:
                    x_copy(s, k).wait()
        for k in range(pieces):
            if s == 0 and c == 0 and not SCALE_FIRST:
                scale(k)
            if s + c < TOGETHER:
                fetched(s, c, k)
                if s > 0 and c == 0:
                    x_copy(s, k).wait()
            term = jnp.dot(xs[s, k], wbuf[s, c, k], preferred_element_type=f32)
            total = term if total is None else total + term
            if s == 0 and c == 0:
                if not SCALE_FIRST:
                    square(k)
                if k == min(BARRIER_AT, pieces - 1):
                    start_queries()
                for o in range(1, mp):
                    if k == min(BARRIER_AT, pieces - 1):
                        for e in range(k + 1):
                            x_copy(o, e).start()
                    elif k > BARRIER_AT:
                        x_copy(o, k).start()
        return total

    if SCALE_FIRST:
        for k in range(pieces):
            scale(k)
            square(k)
    for c in range(2):
        acc[c] = product(0, c)
        if c == 0:
            for s in range(1, mp):
                sum_copy(s).start()

    across = (((1,), (1,)), ((), ()))
    slot = []
    small[1].wait()
    small[2].wait()
    for p in range(passages):
        plan_p = plan[p]

        def count(q, carry):
            end, before = carry
            end = end + counts[q]
            return end, before + jnp.where(end <= plan_p, 1, 0)

        found = lax.fori_loop(0, questions, count, (jnp.int32(0), jnp.int32(0)), unroll=8)[1]
        slot.append(jnp.minimum(found, questions - 1))

    for s in range(1, mp):
        if s == mp - 1:
            for o in range(1, mp):
                sum_copy(o).wait()
            total = sums[0]
            for o in range(1, mp):
                total = total + sums[o]
            high = total.astype(bf16)
            low = (total - high.astype(f32)).astype(bf16)
            both = jnp.concatenate([high, low], axis=1)
            ones = jnp.ones((256, 128), bf16)
            inv_rms = lax.rsqrt(jnp.dot(both, ones, preferred_element_type=f32) * (1.0 / full) + norm_eps)
        for c in range(2):
            total = product(s, c) + acc[c]
            if s < mp - 1:
                acc[c] = total
            elif c == 1:
                kvb[c] = total.astype(bf16)
            else:
                for lanes in range(0, cols, 128):
                    kvb[c, :, lanes:lanes + 128] = (total[:, lanes:lanes + 128] * inv_rms).astype(bf16)

    wide = HEADS_MOST * dec
    row_head = lax.broadcasted_iota(jnp.int32, (wide, cols), 0) // dec
    col_head = lax.broadcasted_iota(jnp.int32, (wide, cols), 1) // HEAD_DIM
    diagonal = row_head == col_head
    stat_row = lax.broadcasted_iota(jnp.int32, (dec, wide), 0)

    def pieces_of(x):
        high = x.astype(bf16).astype(f32)
        rest = x - high
        middle = rest.astype(bf16).astype(f32)
        x = jnp.where(stat_row == 0, high, jnp.where(stat_row == 1, middle, rest - middle))
        return x.astype(bf16)

    own[passages, :, :cols] = jnp.zeros((dec, cols), bf16)
    own[passages, :, cols:] = pieces_of(jnp.full((dec, wide), far_below, f32))

    def pick_own(target):
        at = jnp.int32(passages)
        for p in reversed(range(passages)):
            at = jnp.where(slot[p] == target, p, at)
        return own[at]

    others = qbuf.at[pl.ds(1, dp - 1)]
    pltpu.make_async_copy(others, others, qrecv).wait()

    scores, tops, levels = [], [], []
    for p in range(passages):
        q = qbuf[slot_from(slot[p])].astype(f32)
        q = jnp.where(diagonal, jnp.concatenate([q] * HEADS_MOST, axis=0), 0.0).astype(bf16)
        scores.append(lax.dot_general(
            kvb[0, p * seq:(p + 1) * seq, :], q, across, preferred_element_type=f32) * score_scale)
        levels.append(jnp.max(scores[p], axis=0, keepdims=True))
    for p in range(passages):
        top = levels[p]
        for o in range(passages):
            if o != p:
                top = jnp.where(slot[o] == slot[p], jnp.maximum(top, levels[o]), top)
        tops.append(top)
    w = [jnp.exp(scores[p] - tops[p]) for p in range(passages)]
    dens = [jnp.sum(x, axis=0, keepdims=True) for x in w]
    sums_of = []
    for p in range(passages):
        den = dens[p]
        for o in range(passages):
            if o != p:
                den = den + jnp.where(slot[o] == slot[p], dens[o], 0.0)
        sums_of.append(den)
    nums = []
    for p in range(passages):
        part = w[p] * (1.0 / sums_of[p]) * inv_rms[p * seq:(p + 1) * seq, :wide]
        part = jnp.transpose(part).astype(bf16)
        across_groups = []
        for g in range(groups):
            at = slice(g * width, (g + 1) * width)
            num = jnp.dot(part[g * tall:(g + 1) * tall], kvb[1, p * seq:(p + 1) * seq, at], preferred_element_type=f32)
            num = jnp.where(diagonal[:tall, :width], num, 0.0)
            across_groups.append(jnp.sum(num.reshape(gheads, dec, width), axis=0))
        nums.append(jnp.concatenate(across_groups, axis=1))
    for p in range(passages):
        num = nums[p]
        for o in range(p + 1, passages):
            num = num + jnp.where(slot[o] == slot[p], nums[o], 0.0)
        own[p, :, :cols] = num.astype(bf16)
        own[p, :, cols:] = pieces_of(jnp.broadcast_to(tops[p] + jnp.log(sums_of[p]), (dec, wide)))

    def m_copy(j):
        return pltpu.make_async_remote_copy(
            src_ref=msg.at[j - 1], dst_ref=got.at[j - 1], send_sem=msend, recv_sem=mrecv,
            device_id=(other(j, -1), core), device_id_type=MESH)

    def send(i, carry):
        if M_ORDER == 0:
            j = dp - i
        elif M_ORDER == 1:
            j = slot_to(jnp.where(i - 1 < me, i - 1, i))
        elif M_ORDER == 2:
            j = slot_to(jnp.where(dp - i <= me, dp - i - 1, dp - i))
        elif M_ORDER == 3:
            j = i
        msg[j - 1] = pick_own(other(j, -1))
        m_copy(j).start()
        return carry

    lax.fori_loop(1, dp, send, 0, unroll=5 if dp == 16 else 3)
    got[dp - 1] = pick_own(me)

    pick_row = lax.rem(lax.broadcasted_iota(jnp.int32, (2 * wide, cols), 0), wide) // dec
    pick_col = lax.broadcasted_iota(jnp.int32, (2 * wide, cols), 1) // HEAD_DIM
    pick = jnp.where(pick_row == pick_col, 1.0, 0.0).astype(bf16)
    spread_row = lax.rem(lax.broadcasted_iota(jnp.int32, (dp, dec, wide), 2), dec)
    spread_at = spread_row == lax.broadcasted_iota(jnp.int32, (dp, dec, wide), 1)
    arrived = got.at[pl.ds(0, dp - 1)]
    pltpu.make_async_copy(arrived, arrived, mrecv).wait()
    stat = got[:, :, cols:].astype(f32)
    lse = stat[:, 0:1] + stat[:, 1:2] + stat[:, 2:3]
    top = jnp.max(lse, axis=0, keepdims=True)
    w = jnp.where(lse > 0.5 * far_below, jnp.exp(lse - top), 0.0)
    share = w / jnp.sum(w, axis=0, keepdims=True)
    share = jnp.where(spread_at, share, 0.0).reshape(dp * dec, wide)
    high = share.astype(bf16)
    low = (share - high.astype(f32)).astype(bf16)
    spread = jnp.dot(jnp.concatenate([high, low], axis=1), pick, preferred_element_type=f32)
    nums = got[:, :, :cols].astype(f32)
    out[...] = jnp.sum(spread.reshape(dp, dec, cols) * nums, axis=0).astype(bf16)

    pltpu.make_async_copy(others, others, qsend).wait()
    pltpu.make_async_copy(msg, msg, msend).wait()


BARRIER_AT = 0
WINDOW = 6
FIRST = 6
ROWS_FIRST = True
TOGETHER = 1
M_ORDER = 1
Q_ORDER = 0
SCALE_FIRST = True


def local(dp, mp, store_rows, norm_gain, key_weight, value_weight, queries, counts, slot_plan):
    row_count, feats = store_rows.shape
    cols = key_weight.shape[1]
    width = min(256, cols)
    piece = min(512, feats)
    pieces = feats // piece
    passages = slot_plan.shape[0]
    dec = queries.shape[0]
    questions = counts.shape[0]
    dims = (dp, mp, row_count, feats, cols, piece, width, questions, dec, passages)
    vmem = pl.BlockSpec(memory_space=pltpu.VMEM)
    hbm = pl.BlockSpec(memory_space=pl.ANY)
    dma = pltpu.SemaphoreType.DMA
    line = cols + HEADS_MOST * dec
    return pl.pallas_call(
        functools.partial(body, dims),
        out_shape=jax.ShapeDtypeStruct((dec, cols), bf16),
        in_specs=[hbm] * 7,
        out_specs=vmem,
        scratch_shapes=[
            pltpu.SMEM((questions,), jnp.int32),
            pltpu.SMEM((passages,), jnp.int32),
            pltpu.VMEM((feats * mp,), bf16),
            pltpu.VMEM((pieces, row_count, piece), bf16),
            pltpu.VMEM((mp, pieces, row_count, piece), bf16),
            pltpu.VMEM((mp, 2, pieces, piece, cols), bf16),
            pltpu.VMEM((2, row_count, cols), f32),
            pltpu.VMEM((2, row_count, cols), bf16),
            pltpu.VMEM((mp, row_count, 128), f32),
            pltpu.VMEM((dp, dec, cols), bf16),
            pltpu.VMEM((passages + 1, dec, line), bf16),
            pltpu.VMEM((dp - 1, dec, line), bf16),
            pltpu.VMEM((dp, dec, line), bf16),
            dma((4,)),
            dma((pieces,)),
            dma((mp, 2, pieces)),
            dma((mp, pieces)),
            dma((mp, pieces)),
            dma((mp,)),
            dma((mp,)),
            dma(()),
            dma(()),
            dma(()),
            dma(()),
        ],
        compiler_params=pltpu.CompilerParams(
            collective_id=0, has_side_effects=True, vmem_limit_bytes=56 * 1024 * 1024),
    )(counts, slot_plan, norm_gain, queries, store_rows, key_weight, value_weight)


def solution(mesh):
    placed = (P("dp", "mp"), P(), P(None, "mp"), P(None, "mp"), P("dp", "mp"), P(), P("dp"))
    return jax.shard_map(
        functools.partial(local, mesh.shape["dp"], mesh.shape["mp"]),
        mesh=mesh, in_specs=placed, out_specs=P("dp", "mp"), check_vma=False
    )
```

```python
import functools

import jax
import jax.numpy as jnp
from jax import lax
from jax.experimental import pallas as pl
from jax.experimental.pallas import tpu as pltpu
from jax.sharding import PartitionSpec as P

HEAD_DIM = 64
MESH = pl.DeviceIdType.MESH
bf16, f32 = jnp.bfloat16, jnp.float32

norm_eps = 1e-06
score_scale = 0.125
far_below = -1e30
HEADS_MOST = 16


def body(dims, counts_hbm, plan_hbm, gain_hbm, queries_hbm, rows_hbm, key_hbm, value_hbm, out,
         counts, plan, gain, raw, xs, wbuf, acc, kvb, sums, qbuf, own, msg, got, pick,
         small_sem, rows_sem, w_sem, xsend, xrecv, ssend, srecv, qsend, qrecv, msend, mrecv):
    dp, mp, row_count, feats, cols, piece, width, questions, dec, passages = dims
    full = feats * mp
    seq = row_count // passages
    pieces = feats // piece
    groups = cols // width
    gheads = width // HEAD_DIM
    tall = gheads * dec
    me = lax.axis_index("dp")
    core = lax.axis_index("mp")
    weights = (key_hbm, value_hbm)
    lines = dp // 4
    me_line, me_y, me_x = lax.div(me, 4), lax.rem(lax.div(me, 2), 2), lax.rem(me, 2)

    def other(j, way):
        line = lax.rem(me_line + (lines - j // 4 if way < 0 else j // 4), lines)
        return line * 4 + lax.rem(me_y + j // 2, 2) * 2 + lax.rem(me_x + j, 2)

    def slot_to(target):
        line = lax.rem(me_line - lax.div(target, 4) + lines, lines)
        return line * 4 + lax.rem(lax.rem(lax.div(target, 2), 2) + me_y, 2) * 2 + lax.rem(lax.rem(target, 2) + me_x, 2)

    def slot_from(sender):
        line = lax.rem(lax.div(sender, 4) - me_line + lines, lines)
        return line * 4 + lax.rem(lax.rem(lax.div(sender, 2), 2) + me_y, 2) * 2 + lax.rem(lax.rem(sender, 2) + me_x, 2)

    def rows_copy(k):
        at = pl.ds(k * piece, piece)
        return pltpu.make_async_copy(rows_hbm.at[:, at], raw.at[k], rows_sem.at[k])

    def weight_copy(s, c, k):
        start = pl.multiple_of(lax.rem(core + s, mp) * feats + k * piece, piece)
        return pltpu.make_async_copy(weights[c].at[pl.ds(start, piece), :], wbuf.at[s, c, k], w_sem.at[s, c, k])

    order = [(s, c, k) for s in range(mp) for c in range(2) for k in range(pieces)]

    def fetched(s, c, k):
        weight_copy(s, c, k).wait()
        start_to(order.index((s, c, k)) + 1 + pieces + WINDOW)

    small = [pltpu.make_async_copy(gain_hbm, gain, small_sem.at[0]),
             pltpu.make_async_copy(counts_hbm, counts, small_sem.at[1]),
             pltpu.make_async_copy(plan_hbm, plan, small_sem.at[2])]
    small.append(pltpu.make_async_copy(queries_hbm, qbuf.at[0], small_sem.at[3]))
    small[0].start()
    loads = []
    for k in range(pieces):
        loads += [rows_copy(k), weight_copy(*order[k])]
    if ROWS_FIRST:
        loads = loads[::2] + loads[1::2]
    loads += [weight_copy(*step) for step in order[pieces:]]
    started = [0]

    def start_to(count):
        for copy in loads[started[0]:count]:
            copy.start()
        started[0] = max(started[0], min(count, len(loads)))

    start_to(FIRST)
    barrier = pltpu.get_barrier_semaphore()
    for s in range(1, mp):
        pl.semaphore_signal(barrier, inc=1, device_id=(me, lax.rem(core + s, mp)), device_id_type=MESH)

    def announce(j, carry):
        pl.semaphore_signal(barrier, inc=1, device_id=(other(j, 1), core), device_id_type=MESH)
        return carry

    lax.fori_loop(1, dp, announce, 0, unroll=dp <= 16)
    start_to(SECOND)

    wide = HEADS_MOST * dec
    row_head = lax.broadcasted_iota(jnp.int32, (wide, cols), 0) // dec
    col_head = lax.broadcasted_iota(jnp.int32, (wide, cols), 1) // HEAD_DIM
    diagonal = row_head == col_head
    pick[:wide] = jnp.where(diagonal, 1.0, 0.0).astype(bf16)
    pick[wide:] = jnp.where(diagonal, 1.0, 0.0).astype(bf16)
    start_to(THIRD)
    for copy in small[1:]:
        copy.start()
    stat_row = lax.broadcasted_iota(jnp.int32, (dec, wide), 0)

    def pieces_of(x):
        high = x.astype(bf16).astype(f32)
        rest = x - high
        middle = rest.astype(bf16).astype(f32)
        x = jnp.where(stat_row == 0, high, jnp.where(stat_row == 1, middle, rest - middle))
        return x.astype(bf16)

    own[passages, :, :cols] = jnp.zeros((dec, cols), bf16)
    own[passages, :, cols:] = pieces_of(jnp.full((dec, wide), far_below, f32))

    small[0].wait()

    def scale(k):
        rows_copy(k).wait()
        start_to(THIRD + EACH * (k + 1))
        start = pl.multiple_of(core * feats + k * piece, piece)
        own_gain = gain[pl.ds(start, piece)].reshape(1, piece)
        x = raw[k]
        xs[0, k] = x * own_gain

    def square(k):
        x = raw[k].astype(f32)
        x = x * x
        total = x[:, :128]
        for lanes in range(128, piece, 128):
            total = total + x[:, lanes:lanes + 128]
        sums[0] = total if k == 0 else sums[0] + total

    def x_copy(s, k):
        return pltpu.make_async_remote_copy(
            src_ref=xs.at[0, k], dst_ref=xs.at[s, k], send_sem=xsend.at[s, k], recv_sem=xrecv.at[s, k],
            device_id=(me, lax.rem(core + mp - s, mp)), device_id_type=MESH)

    def sum_copy(s):
        return pltpu.make_async_remote_copy(
            src_ref=sums.at[0], dst_ref=sums.at[s], send_sem=ssend.at[s], recv_sem=srecv.at[s],
            device_id=(me, lax.rem(core + mp - s, mp)), device_id_type=MESH)

    def q_copy(j):
        return pltpu.make_async_remote_copy(
            src_ref=qbuf.at[0], dst_ref=qbuf.at[j], send_sem=qsend, recv_sem=qrecv,
            device_id=(other(j, -1), core), device_id_type=MESH)

    def q_slot(i):
        if Q_ORDER == 0:
            return dp - i
        if Q_ORDER == 1:
            return slot_to(jnp.where(i - 1 < me, i - 1, i))
        if Q_ORDER == 2:
            return slot_to(jnp.where(dp - i <= me, dp - i - 1, dp - i))
        return (lines - 1 - (dp - i) // 4) * 4 + 4 + (dp - i) % 4 if (dp - i) >= 4 else dp - i

    def start_queries():
        small[3].wait()
        pl.semaphore_wait(barrier, dp - 1 + mp - 1)
        lax.fori_loop(1, dp, lambda j, carry: (q_copy(q_slot(j)).start(), carry)[1], 0, unroll=dp <= 16)

    def product(s, c, between=None):
        total = None
        if s + c >= TOGETHER:
            for k in range(pieces):
                fetched(s, c, k)
                if s > 0 and c == 0:
                    x_copy(s, k).wait()
        if between is not None:
            between()
        for k in range(pieces):
            if s == 0 and c == 0 and not SCALE_FIRST:
                scale(k)
            if s + c < TOGETHER:
                fetched(s, c, k)
                if s > 0 and c == 0:
                    x_copy(s, k).wait()
            term = jnp.dot(xs[s, k], wbuf[s, c, k], preferred_element_type=f32)
            total = term if total is None else total + term
            if s == 0 and c == 0:
                if not SCALE_FIRST:
                    square(k)
                if k == min(BARRIER_AT, pieces - 1):
                    start_queries()
                for o in range(1, mp):
                    if k == min(BARRIER_AT, pieces - 1):
                        for e in range(k + 1):
                            x_copy(o, e).start()
                    elif k > BARRIER_AT:
                        x_copy(o, k).start()
        return total

    if SCALE_FIRST:
        for k in range(pieces):
            scale(k)
            square(k)
    for c in range(2):
        acc[c] = product(0, c)
        if c == 0:
            for s in range(1, mp):
                sum_copy(s).start()

    across = (((1,), (1,)), ((), ()))
    slot = []
    small[1].wait()
    small[2].wait()
    for p in range(passages):
        plan_p = plan[p]

        def count(q, carry):
            end, before = carry
            end = end + counts[q]
            return end, before + jnp.where(end <= plan_p, 1, 0)

        found = lax.fori_loop(0, questions, count, (jnp.int32(0), jnp.int32(0)), unroll=8)[1]
        slot.append(jnp.minimum(found, questions - 1))

    others = qbuf.at[pl.ds(1, dp - 1)]

    def score():
        pltpu.make_async_copy(others, others, qrecv).wait()

        scores, tops, levels = [], [], []
        for p in range(passages):
            q = qbuf[slot_from(slot[p])]
            q = jnp.concatenate([q] * HEADS_MOST, axis=0) * pick[:wide]
            scores.append(lax.dot_general(
                kvb[0, p * seq:(p + 1) * seq, :], q, across, preferred_element_type=f32) * score_scale)
            levels.append(jnp.max(scores[p], axis=0, keepdims=True))
        for p in range(passages):
            top = levels[p]
            for o in range(passages):
                if o != p:
                    top = jnp.where(slot[o] == slot[p], jnp.maximum(top, levels[o]), top)
            tops.append(top)
        w = [jnp.exp(scores[p] - tops[p]) for p in range(passages)]
        dens = [jnp.sum(x, axis=0, keepdims=True) for x in w]
        sums_of = []
        for p in range(passages):
            den = dens[p]
            for o in range(passages):
                if o != p:
                    den = den + jnp.where(slot[o] == slot[p], dens[o], 0.0)
            sums_of.append(den)
        return w, tops, sums_of

    for s in range(1, mp):
        if s == mp - 1:
            for o in range(1, mp):
                sum_copy(o).wait()
            total = sums[0]
            for o in range(1, mp):
                total = total + sums[o]
            high = total.astype(bf16)
            low = (total - high.astype(f32)).astype(bf16)
            both = jnp.concatenate([high, low], axis=1)
            ones = jnp.ones((256, 128), bf16)
            inv_rms = lax.rsqrt(jnp.dot(both, ones, preferred_element_type=f32) * (1.0 / full) + norm_eps)
        for c in range(2):
            between = []
            total = product(s, c, (lambda: between.append(score())) if s == mp - 1 and c == 1 else None) + acc[c]
            if between:
                w, tops, sums_of = between[0]
            if s < mp - 1:
                acc[c] = total
            elif c == 1:
                kvb[c] = total.astype(bf16)
            else:
                for lanes in range(0, cols, 128):
                    kvb[c, :, lanes:lanes + 128] = (total[:, lanes:lanes + 128] * inv_rms).astype(bf16)

    def pick_own(target):
        at = jnp.int32(passages)
        for p in reversed(range(passages)):
            at = jnp.where(slot[p] == target, p, at)
        return own[at]

    nums = []
    for p in range(passages):
        part = w[p] * (1.0 / sums_of[p]) * inv_rms[p * seq:(p + 1) * seq, :wide]
        part = jnp.transpose(part).astype(bf16)
        across_groups = []
        for g in range(groups):
            at = slice(g * width, (g + 1) * width)
            num = jnp.dot(part[g * tall:(g + 1) * tall], kvb[1, p * seq:(p + 1) * seq, at], preferred_element_type=f32)
            num = jnp.where(diagonal[:tall, :width], num, 0.0)
            across_groups.append(jnp.sum(num.reshape(gheads, dec, width), axis=0))
        nums.append(jnp.concatenate(across_groups, axis=1))
    for p in range(passages):
        num = nums[p]
        for o in range(p + 1, passages):
            num = num + jnp.where(slot[o] == slot[p], nums[o], 0.0)
        own[p, :, :cols] = num.astype(bf16)
        own[p, :, cols:] = pieces_of(jnp.broadcast_to(tops[p] + jnp.log(sums_of[p]), (dec, wide)))

    def m_copy(j):
        return pltpu.make_async_remote_copy(
            src_ref=msg.at[j - 1], dst_ref=got.at[j - 1], send_sem=msend, recv_sem=mrecv,
            device_id=(other(j, -1), core), device_id_type=MESH)

    def send(i, carry):
        if M_ORDER == 0:
            j = dp - i
        elif M_ORDER == 1:
            j = slot_to(jnp.where(i - 1 < me, i - 1, i))
        elif M_ORDER == 2:
            j = slot_to(jnp.where(dp - i <= me, dp - i - 1, dp - i))
        elif M_ORDER == 3:
            j = i
        msg[j - 1] = pick_own(other(j, -1))
        m_copy(j).start()
        return carry

    lax.fori_loop(1, dp, send, 0, unroll=5 if dp == 16 else 3)
    got[dp - 1] = pick_own(me)

    spread_row = lax.rem(lax.broadcasted_iota(jnp.int32, (dp, dec, wide), 2), dec)
    spread_at = spread_row == lax.broadcasted_iota(jnp.int32, (dp, dec, wide), 1)
    arrived = got.at[pl.ds(0, dp - 1)]
    pltpu.make_async_copy(arrived, arrived, mrecv).wait()
    stat = got[:, :, cols:].astype(f32)
    lse = stat[:, 0:1] + stat[:, 1:2] + stat[:, 2:3]
    top = jnp.max(lse, axis=0, keepdims=True)
    w = jnp.where(lse > 0.5 * far_below, jnp.exp(lse - top), 0.0)
    share = w / jnp.sum(w, axis=0, keepdims=True)
    share = jnp.where(spread_at, share, 0.0).reshape(dp * dec, wide)
    high = share.astype(bf16)
    low = (share - high.astype(f32)).astype(bf16)
    spread = jnp.dot(jnp.concatenate([high, low], axis=1), pick[...], preferred_element_type=f32)
    nums = got[:, :, :cols].astype(f32)
    out[...] = jnp.sum(spread.reshape(dp, dec, cols) * nums, axis=0).astype(bf16)

    pltpu.make_async_copy(others, others, qsend).wait()
    pltpu.make_async_copy(msg, msg, msend).wait()


BARRIER_AT = 0
WINDOW = 6
FIRST = 6
SECOND = 6
THIRD = 6
EACH = 1
ROWS_FIRST = True
TOGETHER = 1
M_ORDER = 1
Q_ORDER = 0
SCALE_FIRST = True


def local(dp, mp, store_rows, norm_gain, key_weight, value_weight, queries, counts, slot_plan):
    row_count, feats = store_rows.shape
    cols = key_weight.shape[1]
    width = min(256, cols)
    piece = min(512, feats)
    pieces = feats // piece
    passages = slot_plan.shape[0]
    dec = queries.shape[0]
    questions = counts.shape[0]
    dims = (dp, mp, row_count, feats, cols, piece, width, questions, dec, passages)
    vmem = pl.BlockSpec(memory_space=pltpu.VMEM)
    hbm = pl.BlockSpec(memory_space=pl.ANY)
    dma = pltpu.SemaphoreType.DMA
    line = cols + HEADS_MOST * dec
    return pl.pallas_call(
        functools.partial(body, dims),
        out_shape=jax.ShapeDtypeStruct((dec, cols), bf16),
        in_specs=[hbm] * 7,
        out_specs=vmem,
        scratch_shapes=[
            pltpu.SMEM((questions,), jnp.int32),
            pltpu.SMEM((passages,), jnp.int32),
            pltpu.VMEM((feats * mp,), bf16),
            pltpu.VMEM((pieces, row_count, piece), bf16),
            pltpu.VMEM((mp, pieces, row_count, piece), bf16),
            pltpu.VMEM((mp, 2, pieces, piece, cols), bf16),
            pltpu.VMEM((2, row_count, cols), f32),
            pltpu.VMEM((2, row_count, cols), bf16),
            pltpu.VMEM((mp, row_count, 128), f32),
            pltpu.VMEM((dp, dec, cols), bf16),
            pltpu.VMEM((passages + 1, dec, line), bf16),
            pltpu.VMEM((dp - 1, dec, line), bf16),
            pltpu.VMEM((dp, dec, line), bf16),
            pltpu.VMEM((2 * HEADS_MOST * dec, cols), bf16),
            dma((4,)),
            dma((pieces,)),
            dma((mp, 2, pieces)),
            dma((mp, pieces)),
            dma((mp, pieces)),
            dma((mp,)),
            dma((mp,)),
            dma(()),
            dma(()),
            dma(()),
            dma(()),
        ],
        compiler_params=pltpu.CompilerParams(
            collective_id=0, has_side_effects=True, vmem_limit_bytes=56 * 1024 * 1024),
    )(counts, slot_plan, norm_gain, queries, store_rows, key_weight, value_weight)


def solution(mesh):
    placed = (P("dp", "mp"), P(), P(None, "mp"), P(None, "mp"), P("dp", "mp"), P(), P("dp"))
    return jax.shard_map(
        functools.partial(local, mesh.shape["dp"], mesh.shape["mp"]),
        mesh=mesh, in_specs=placed, out_specs=P("dp", "mp"), check_vma=False
    )
```

```python
import functools

import jax
import jax.numpy as jnp
from jax import lax
from jax.experimental import pallas as pl
from jax.experimental.pallas import tpu as pltpu
from jax.sharding import PartitionSpec as P

HEAD_DIM = 64
MESH = pl.DeviceIdType.MESH
bf16, f32 = jnp.bfloat16, jnp.float32

norm_eps = 1e-06
score_scale = 0.125
far_below = -1e30
HEADS_MOST = 16


def body(dims, counts_hbm, plan_hbm, gain_hbm, queries_hbm, rows_hbm, key_hbm, value_hbm, out,
         counts, plan, gain, raw, xs, wbuf, acc, kvb, sums, qbuf, own, msg, got, pick,
         small_sem, rows_sem, w_sem, xsend, xrecv, ssend, srecv, qsend, qrecv, msend, mrecv):
    dp, mp, row_count, feats, cols, piece, width, questions, dec, passages = dims
    full = feats * mp
    seq = row_count // passages
    pieces = feats // piece
    groups = cols // width
    gheads = width // HEAD_DIM
    tall = gheads * dec
    me = lax.axis_index("dp")
    core = lax.axis_index("mp")
    weights = (key_hbm, value_hbm)
    lines = dp // 4
    me_line, me_y, me_x = lax.div(me, 4), lax.rem(lax.div(me, 2), 2), lax.rem(me, 2)

    def other(j, way):
        line = lax.rem(me_line + (lines - j // 4 if way < 0 else j // 4), lines)
        return line * 4 + lax.rem(me_y + j // 2, 2) * 2 + lax.rem(me_x + j, 2)

    def slot_to(target):
        line = lax.rem(me_line - lax.div(target, 4) + lines, lines)
        return line * 4 + lax.rem(lax.rem(lax.div(target, 2), 2) + me_y, 2) * 2 + lax.rem(lax.rem(target, 2) + me_x, 2)

    def slot_from(sender):
        line = lax.rem(lax.div(sender, 4) - me_line + lines, lines)
        return line * 4 + lax.rem(lax.rem(lax.div(sender, 2), 2) + me_y, 2) * 2 + lax.rem(lax.rem(sender, 2) + me_x, 2)

    def rows_copy(k):
        at = pl.ds(k * piece, piece)
        return pltpu.make_async_copy(rows_hbm.at[:, at], raw.at[k], rows_sem.at[k])

    def weight_copy(s, c, k):
        start = pl.multiple_of(lax.rem(core + s, mp) * feats + k * piece, piece)
        return pltpu.make_async_copy(weights[c].at[pl.ds(start, piece), :], wbuf.at[s, c, k], w_sem.at[s, c, k])

    order = [(s, c, k) for s in range(mp) for c in range(2) for k in range(pieces)]

    def fetched(s, c, k):
        weight_copy(s, c, k).wait()
        start_to(order.index((s, c, k)) + 1 + pieces + WINDOW)

    small = [pltpu.make_async_copy(gain_hbm, gain, small_sem.at[0]),
             pltpu.make_async_copy(counts_hbm, counts, small_sem.at[1]),
             pltpu.make_async_copy(plan_hbm, plan, small_sem.at[2])]
    small.append(pltpu.make_async_copy(queries_hbm, qbuf.at[0], small_sem.at[3]))
    small[0].start()
    loads = []
    for k in range(pieces):
        loads += [rows_copy(k), weight_copy(*order[k])]
    if ROWS_FIRST:
        loads = loads[::2] + loads[1::2]
    loads += [weight_copy(*step) for step in order[pieces:]]
    started = [0]

    def start_to(count):
        for copy in loads[started[0]:count]:
            copy.start()
        started[0] = max(started[0], min(count, len(loads)))

    start_to(FIRST)
    barrier = pltpu.get_barrier_semaphore()
    for s in range(1, mp):
        pl.semaphore_signal(barrier, inc=1, device_id=(me, lax.rem(core + s, mp)), device_id_type=MESH)

    def announce(j, carry):
        pl.semaphore_signal(barrier, inc=1, device_id=(other(j, 1), core), device_id_type=MESH)
        return carry

    lax.fori_loop(1, dp, announce, 0, unroll=dp <= 16)
    start_to(SECOND)

    wide = HEADS_MOST * dec
    row_head = lax.broadcasted_iota(jnp.int32, (wide, cols), 0) // dec
    col_head = lax.broadcasted_iota(jnp.int32, (wide, cols), 1) // HEAD_DIM
    diagonal = row_head == col_head
    pick[:wide] = jnp.where(diagonal, 1.0, 0.0).astype(bf16)
    pick[wide:] = jnp.where(diagonal, 1.0, 0.0).astype(bf16)
    start_to(THIRD)
    for copy in small[1:]:
        copy.start()
    stat_row = lax.broadcasted_iota(jnp.int32, (dec, wide), 0)

    def pieces_of(x):
        high = x.astype(bf16).astype(f32)
        rest = x - high
        middle = rest.astype(bf16).astype(f32)
        x = jnp.where(stat_row == 0, high, jnp.where(stat_row == 1, middle, rest - middle))
        return x.astype(bf16)

    own[passages, :, :cols] = jnp.zeros((dec, cols), bf16)
    own[passages, :, cols:] = pieces_of(jnp.full((dec, wide), far_below, f32))

    small[0].wait()

    def scale(k):
        rows_copy(k).wait()
        start_to(THIRD + EACH * (k + 1))
        start = pl.multiple_of(core * feats + k * piece, piece)
        own_gain = gain[pl.ds(start, piece)].reshape(1, piece)
        x = raw[k]
        xs[0, k] = x * own_gain

    def square(k):
        x = raw[k].astype(f32)
        x = x * x
        total = x[:, :128]
        for lanes in range(128, piece, 128):
            total = total + x[:, lanes:lanes + 128]
        sums[0] = total if k == 0 else sums[0] + total

    def x_copy(s, k):
        return pltpu.make_async_remote_copy(
            src_ref=xs.at[0, k], dst_ref=xs.at[s, k], send_sem=xsend.at[s, k], recv_sem=xrecv.at[s, k],
            device_id=(me, lax.rem(core + mp - s, mp)), device_id_type=MESH)

    def sum_copy(s):
        return pltpu.make_async_remote_copy(
            src_ref=sums.at[0], dst_ref=sums.at[s], send_sem=ssend.at[s], recv_sem=srecv.at[s],
            device_id=(me, lax.rem(core + mp - s, mp)), device_id_type=MESH)

    def q_copy(j):
        return pltpu.make_async_remote_copy(
            src_ref=qbuf.at[0], dst_ref=qbuf.at[j], send_sem=qsend, recv_sem=qrecv,
            device_id=(other(j, -1), core), device_id_type=MESH)

    def q_slot(i):
        if Q_ORDER == 0:
            return dp - i
        if Q_ORDER == 1:
            return slot_to(jnp.where(i - 1 < me, i - 1, i))
        if Q_ORDER == 2:
            return slot_to(jnp.where(dp - i <= me, dp - i - 1, dp - i))
        return (lines - 1 - (dp - i) // 4) * 4 + 4 + (dp - i) % 4 if (dp - i) >= 4 else dp - i

    def start_queries():
        small[3].wait()
        pl.semaphore_wait(barrier, dp - 1 + mp - 1)
        lax.fori_loop(1, dp, lambda j, carry: (q_copy(q_slot(j)).start(), carry)[1], 0, unroll=dp <= 16)

    def product(s, c, between=None):
        total = None
        if s + c >= TOGETHER:
            for k in range(pieces):
                fetched(s, c, k)
                if s > 0 and c == 0:
                    x_copy(s, k).wait()
        if between is not None:
            between()
        for k in range(pieces):
            if s == 0 and c == 0 and not SCALE_FIRST:
                scale(k)
            if s + c < TOGETHER:
                fetched(s, c, k)
                if s > 0 and c == 0:
                    x_copy(s, k).wait()
            term = jnp.dot(xs[s, k], wbuf[s, c, k], preferred_element_type=f32)
            total = term if total is None else total + term
            if s == 0 and c == 0:
                if not SCALE_FIRST:
                    square(k)
                if k == min(BARRIER_AT, pieces - 1):
                    start_queries()
                for o in range(1, mp):
                    if k == min(BARRIER_AT, pieces - 1):
                        for e in range(k + 1):
                            x_copy(o, e).start()
                    elif k > BARRIER_AT:
                        x_copy(o, k).start()
        return total

    slot = []
    small[1].wait()
    small[2].wait()
    for p in range(passages):
        plan_p = plan[p]

        def count(q, carry):
            end, before = carry
            end = end + counts[q]
            return end, before + jnp.where(end <= plan_p, 1, 0)

        found = lax.fori_loop(0, questions, count, (jnp.int32(0), jnp.int32(0)), unroll=8)[1]
        slot.append(jnp.minimum(found, questions - 1))

    if SCALE_FIRST:
        for k in range(pieces):
            scale(k)
            square(k)
    for c in range(2):
        acc[c] = product(0, c)
        if c == 0:
            for s in range(1, mp):
                sum_copy(s).start()

    across = (((1,), (1,)), ((), ()))
    others = qbuf.at[pl.ds(1, dp - 1)]

    def score():
        pltpu.make_async_copy(others, others, qrecv).wait()

        scores, tops, levels = [], [], []
        for p in range(passages):
            q = qbuf[slot_from(slot[p])]
            q = jnp.concatenate([q] * HEADS_MOST, axis=0) * pick[:wide]
            scores.append(lax.dot_general(
                kvb[0, p * seq:(p + 1) * seq, :], q, across, preferred_element_type=f32) * score_scale)
            levels.append(jnp.max(scores[p], axis=0, keepdims=True))
        for p in range(passages):
            top = levels[p]
            for o in range(passages):
                if o != p:
                    top = jnp.where(slot[o] == slot[p], jnp.maximum(top, levels[o]), top)
            tops.append(top)
        w = [jnp.exp(scores[p] - tops[p]) for p in range(passages)]
        dens = [jnp.sum(x, axis=0, keepdims=True) for x in w]
        sums_of = []
        for p in range(passages):
            den = dens[p]
            for o in range(passages):
                if o != p:
                    den = den + jnp.where(slot[o] == slot[p], dens[o], 0.0)
            sums_of.append(den)
        return w, tops, sums_of

    for s in range(1, mp):
        if s == mp - 1:
            for o in range(1, mp):
                sum_copy(o).wait()
            total = sums[0]
            for o in range(1, mp):
                total = total + sums[o]
            high = total.astype(bf16)
            low = (total - high.astype(f32)).astype(bf16)
            both = jnp.concatenate([high, low], axis=1)
            ones = jnp.ones((256, 128), bf16)
            inv_rms = lax.rsqrt(jnp.dot(both, ones, preferred_element_type=f32) * (1.0 / full) + norm_eps)
        for c in range(2):
            between = []
            total = product(s, c, (lambda: between.append(score())) if s == mp - 1 and c == 1 else None) + acc[c]
            if between:
                w, tops, sums_of = between[0]
            if s < mp - 1:
                acc[c] = total
            elif c == 1:
                kvb[c] = total.astype(bf16)
            else:
                for lanes in range(0, cols, 128):
                    kvb[c, :, lanes:lanes + 128] = (total[:, lanes:lanes + 128] * inv_rms).astype(bf16)

    def pick_own(target):
        at = jnp.int32(passages)
        for p in reversed(range(passages)):
            at = jnp.where(slot[p] == target, p, at)
        return own[at]

    nums = []
    for p in range(passages):
        part = w[p] * (1.0 / sums_of[p]) * inv_rms[p * seq:(p + 1) * seq, :wide]
        part = jnp.transpose(part).astype(bf16)
        across_groups = []
        for g in range(groups):
            at = slice(g * width, (g + 1) * width)
            num = jnp.dot(part[g * tall:(g + 1) * tall], kvb[1, p * seq:(p + 1) * seq, at], preferred_element_type=f32)
            num = jnp.where(diagonal[:tall, :width], num, 0.0)
            across_groups.append(jnp.sum(num.reshape(gheads, dec, width), axis=0))
        nums.append(jnp.concatenate(across_groups, axis=1))
    for p in range(passages):
        num = nums[p]
        for o in range(p + 1, passages):
            num = num + jnp.where(slot[o] == slot[p], nums[o], 0.0)
        own[p, :, :cols] = num.astype(bf16)
        own[p, :, cols:] = pieces_of(jnp.broadcast_to(tops[p] + jnp.log(sums_of[p]), (dec, wide)))

    def m_copy(j):
        return pltpu.make_async_remote_copy(
            src_ref=msg.at[j - 1], dst_ref=got.at[j - 1], send_sem=msend, recv_sem=mrecv,
            device_id=(other(j, -1), core), device_id_type=MESH)

    def send(i, carry):
        if M_ORDER == 0:
            j = dp - i
        elif M_ORDER == 1:
            j = slot_to(jnp.where(i - 1 < me, i - 1, i))
        elif M_ORDER == 2:
            j = slot_to(jnp.where(dp - i <= me, dp - i - 1, dp - i))
        elif M_ORDER == 3:
            j = i
        msg[j - 1] = pick_own(other(j, -1))
        m_copy(j).start()
        return carry

    lax.fori_loop(1, dp, send, 0, unroll=5 if dp == 16 else 3)
    got[dp - 1] = pick_own(me)

    spread_row = lax.rem(lax.broadcasted_iota(jnp.int32, (dp, dec, wide), 2), dec)
    spread_at = spread_row == lax.broadcasted_iota(jnp.int32, (dp, dec, wide), 1)
    arrived = got.at[pl.ds(0, dp - 1)]
    pltpu.make_async_copy(arrived, arrived, mrecv).wait()
    stat = got[:, :, cols:].astype(f32)
    lse = stat[:, 0:1] + stat[:, 1:2] + stat[:, 2:3]
    top = jnp.max(lse, axis=0, keepdims=True)
    w = jnp.where(lse > 0.5 * far_below, jnp.exp(lse - top), 0.0)
    share = w / jnp.sum(w, axis=0, keepdims=True)
    share = jnp.where(spread_at, share, 0.0).reshape(dp * dec, wide)
    high = share.astype(bf16)
    low = (share - high.astype(f32)).astype(bf16)
    spread = jnp.dot(jnp.concatenate([high, low], axis=1), pick[...], preferred_element_type=f32)
    nums = got[:, :, :cols].astype(f32)
    out[...] = jnp.sum(spread.reshape(dp, dec, cols) * nums, axis=0).astype(bf16)

    pltpu.make_async_copy(others, others, qsend).wait()
    pltpu.make_async_copy(msg, msg, msend).wait()


BARRIER_AT = 0
WINDOW = 6
FIRST = 6
SECOND = 6
THIRD = 6
EACH = 1
ROWS_FIRST = True
TOGETHER = 1
M_ORDER = 1
Q_ORDER = 0
SCALE_FIRST = True


def local(dp, mp, store_rows, norm_gain, key_weight, value_weight, queries, counts, slot_plan):
    row_count, feats = store_rows.shape
    cols = key_weight.shape[1]
    width = min(256, cols)
    piece = min(512, feats)
    pieces = feats // piece
    passages = slot_plan.shape[0]
    dec = queries.shape[0]
    questions = counts.shape[0]
    dims = (dp, mp, row_count, feats, cols, piece, width, questions, dec, passages)
    vmem = pl.BlockSpec(memory_space=pltpu.VMEM)
    hbm = pl.BlockSpec(memory_space=pl.ANY)
    dma = pltpu.SemaphoreType.DMA
    line = cols + HEADS_MOST * dec
    return pl.pallas_call(
        functools.partial(body, dims),
        out_shape=jax.ShapeDtypeStruct((dec, cols), bf16),
        in_specs=[hbm] * 7,
        out_specs=vmem,
        scratch_shapes=[
            pltpu.SMEM((questions,), jnp.int32),
            pltpu.SMEM((passages,), jnp.int32),
            pltpu.VMEM((feats * mp,), bf16),
            pltpu.VMEM((pieces, row_count, piece), bf16),
            pltpu.VMEM((mp, pieces, row_count, piece), bf16),
            pltpu.VMEM((mp, 2, pieces, piece, cols), bf16),
            pltpu.VMEM((2, row_count, cols), f32),
            pltpu.VMEM((2, row_count, cols), bf16),
            pltpu.VMEM((mp, row_count, 128), f32),
            pltpu.VMEM((dp, dec, cols), bf16),
            pltpu.VMEM((passages + 1, dec, line), bf16),
            pltpu.VMEM((dp - 1, dec, line), bf16),
            pltpu.VMEM((dp, dec, line), bf16),
            pltpu.VMEM((2 * HEADS_MOST * dec, cols), bf16),
            dma((4,)),
            dma((pieces,)),
            dma((mp, 2, pieces)),
            dma((mp, pieces)),
            dma((mp, pieces)),
            dma((mp,)),
            dma((mp,)),
            dma(()),
            dma(()),
            dma(()),
            dma(()),
        ],
        compiler_params=pltpu.CompilerParams(
            collective_id=0, has_side_effects=True, vmem_limit_bytes=56 * 1024 * 1024),
    )(counts, slot_plan, norm_gain, queries, store_rows, key_weight, value_weight)


def solution(mesh):
    placed = (P("dp", "mp"), P(), P(None, "mp"), P(None, "mp"), P("dp", "mp"), P(), P("dp"))
    return jax.shard_map(
        functools.partial(local, mesh.shape["dp"], mesh.shape["mp"]),
        mesh=mesh, in_specs=placed, out_specs=P("dp", "mp"), check_vma=False
    )
```
